32 devices in a mesh: groups: 2 (over y), chan: 4 (over z), img: 4 (over x, core).
Axes of the slice: x: 2, y: 2, z: 4, core: 2. Of those that a mesh axis runs over, the one named last changes fastest.
Arguments:
- features: bfloat16 [8, 16, 16, 2048], P(('groups', 'img'), None, None, 'chan'), parts along dimension 0, may hold values from -6 to 6
- kernel_one: bfloat16 [3, 3, 2048, 2048], P(None, None, 'img', 'chan'), may hold values from -0.046875 to 0.046875
- kernel_two: bfloat16 [3, 3, 2048, 2048], P(None, None, 'img', 'chan'), may hold values from -0.046875 to 0.046875
Outputs:
- second_out: bfloat16 [8, 16, 16, 2048], P(('groups', 'img'), None, None, 'chan'), parts along dimension 0
The draws below stay inside these ranges and needn't reach their ends.
There are 2 independent parts, one for each index of `groups`. The reference program is written for one: setup_inputs(seed, part) draws one part's arguments, and reference() takes and returns one part's arrays. A program takes and returns all parts, laid end to end along the dimension named above; an argument that names none is the same for every part. Nothing has to cross between parts.
All inputs are finite; a program needn't handle non-finite values.
Results may differ from the reference program's by a relative error of at most 0.005.
Values may be sent and summed in bfloat16 or wider, within the bound.
A program may use at most 64 MiB of HBM per device.

```python
import jax
import jax.numpy as jnp

C = 2048
IMG_H = 16
IMG_W = 16
FRAMES = 4


def steps_of(stream_key, shape, split, low, high):
    def one(axis_at, parts):
        draws = jax.random.uniform(jax.random.fold_in(jax.random.fold_in(stream_key, 6), axis_at), (parts,), jnp.float32, low / len(split), high / len(split))
        return jnp.repeat(jnp.exp(draws), shape[axis_at] // parts).reshape((-1,) + (1,) * (len(shape) - axis_at - 1))

    level = one(*split[0])
    for cut in split[1:]:
        level = level * one(*cut)
    return level


def bell_draw(own_key, dims, scale, limit, cuts=(), held_as=jnp.bfloat16):
    values = scale * jax.random.normal(own_key, dims, jnp.float32)
    if cuts:
        values = values * steps_of(own_key, dims, cuts, -0.22, 0.18)
    return jnp.clip(values, -limit, limit).astype(held_as)


def setup_inputs(seed: int = 0, part: int = 0) -> dict:
    keys = jax.random.split(jax.random.key(seed), 4)
    part_splits = jax.random.split(jax.random.fold_in(keys[3], part), 4)
    features = bell_draw(part_splits[0], (FRAMES, IMG_H, IMG_W, C), 1.0, 6.0, ((0, 4), (3, 4)))
    kernel_one = bell_draw(keys[1], (3, 3, C, C), (9 * C) ** -0.5, 0.046875, ((2, 4), (3, 4)))
    kernel_two = bell_draw(keys[2], (3, 3, C, C), (9 * C) ** -0.5, 0.046875, ((2, 4), (3, 4)))
    return {"features": features, "kernel_one": kernel_one, "kernel_two": kernel_two}


def pad_frames(active):
    return jnp.pad(active, ((0, 0), (1, 1), (1, 1), (0, 0)))


def conv_padded(padded, kernel):
    frame_count = padded.shape[0]
    height = padded.shape[1] - 2
    breadth = padded.shape[2] - 2
    summed = jnp.zeros((frame_count * height * breadth, kernel.shape[3]), jnp.float32)
    for offset_y in range(3):
        for offset_x in range(3):
            window = padded[:, offset_y:offset_y + height, offset_x:offset_x + breadth, :]
            window = window.reshape(frame_count * height * breadth, padded.shape[3])
            summed = summed + jnp.dot(window, kernel[offset_y, offset_x], preferred_element_type=jnp.float32)
    return summed.reshape(frame_count, height, breadth, kernel.shape[3])


def reference(features, kernel_one, kernel_two):
    first = conv_padded(pad_frames(features), kernel_one)
    hidden = jax.nn.silu(first).astype(jnp.bfloat16)
    return conv_padded(pad_frames(hidden), kernel_two).astype(jnp.bfloat16)
```

```python
import functools

import jax
import jax.numpy as jnp
from jax import lax
from jax.experimental import pallas as pl
from jax.experimental.pallas import tpu as pltpu
from jax.sharding import PartitionSpec as P

MESH = pl.DeviceIdType.MESH
F32 = jnp.float32
BF16 = jnp.bfloat16


def kernel(
    nx, m, H, W,
    x_ref, k1_ref, k2_ref, out_ref,
    w, hid, GU, GD, A, X3, F, SP, SS, R1, R2,
    wsem, us, ds, ur, dr, sps, ar, s1, r1, s2, r2,
):
    n = 2 * nx
    HW, ct = x_ref.shape
    ci = w.shape[1] // 9
    k = ci // ct
    me = lax.axis_index("img")
    z = lax.axis_index("chan")
    mx, core = me // 2, me % 2

    def frame(d):
        return lax.rem(mx + d // 2, nx) * 2 + (lax.rem(core + 1, 2) if d % 2 else core)

    def to(i=None, c=None):
        return {"img": me if i is None else i, "chan": z if c is None else c}

    wcopies = [pltpu.make_async_copy(kr, w.at[l], wsem.at[l]) for l, kr in enumerate((k1_ref, k2_ref))]
    for cp in wcopies:
        cp.start()

    bar = pltpu.get_barrier_semaphore()
    for d in range(1, n):
        pl.semaphore_signal(bar, inc=1, device_id=to(i=frame(d)), device_id_type=MESH)

    @pl.when(z > 0)
    def _():
        pl.semaphore_signal(bar, inc=1, device_id=to(c=z - 1), device_id_type=MESH)

    @pl.when(z < m - 1)
    def _():
        pl.semaphore_signal(bar, inc=1, device_id=to(c=z + 1), device_id_type=MESH)

    X3[:, 0:W, :] = jnp.zeros((n, W, 3 * ci), BF16)
    X3[:, (H + 1) * W : (H + 2) * W, :] = jnp.zeros((n, W, 3 * ci), BF16)
    pl.semaphore_wait(bar, n - 1 + jnp.where(z > 0, 1, 0) + jnp.where(z < m - 1, 1, 0))

    def rdma(src, dst, ss, rs, dev):
        return pltpu.make_async_remote_copy(
            src_ref=src, dst_ref=dst, send_sem=ss, recv_sem=rs, device_id=dev, device_id_type=MESH
        )

    def up(l, t, src):
        return rdma(src, GU.at[l, t], us.at[l, t], ur.at[l, t], to(c=z + 1))

    def down(l, t, src):
        return rdma(src, GD.at[l, t], ds.at[l, t], dr.at[l, t], to(c=z - 1))

    def spread_copy(l, q, src, s):
        return rdma(src, A.at[l, me, s % k], sps.at[l, q], ar.at[l, me, s % k], to(i=s // k))

    def spread(l, q, src, s):
        @pl.when(s // k != me)
        def _():
            spread_copy(l, q, src, s).start()

        @pl.when(s // k == me)
        def _():
            A[l, me, s % k] = src[...]

    def gather(l, src):
        @pl.when(z < m - 1)
        def _():
            up(l, 0, src).start()

        @pl.when(z > 0)
        def _():
            down(l, 0, src).start()

        spread(l, 0, src, z)
        for t in range(m - 1):
            @pl.when(z > t)
            def _():
                up(l, t, src).wait_recv()
                if t < m - 2:
                    @pl.when(z < m - 1)
                    def _():
                        up(l, t + 1, GU.at[l, t]).start()
                spread(l, 1 + t, GU.at[l, t], z - 1 - t)

            @pl.when(z + 1 + t < m)
            def _():
                down(l, t, src).wait_recv()
                if t < m - 2:
                    @pl.when(z > 0)
                    def _():
                        down(l, t + 1, GD.at[l, t]).start()
                spread(l, m + t, GD.at[l, t], z + 1 + t)

    def gather_sends(l, src):
        @pl.when(z < m - 1)
        def _():
            up(l, 0, src).wait_send()

        @pl.when(z > 0)
        def _():
            down(l, 0, src).wait_send()

        @pl.when(z // k != me)
        def _():
            spread_copy(l, 0, src, z).wait_send()

        for t in range(m - 1):
            if t < m - 2:
                @pl.when((z > t) & (z < m - 1))
                def _():
                    up(l, t + 1, GU.at[l, t]).wait_send()

                @pl.when((z + 1 + t < m) & (z > 0))
                def _():
                    down(l, t + 1, GD.at[l, t]).wait_send()

            @pl.when((z > t) & ((z - 1 - t) // k != me))
            def _():
                spread_copy(l, 1 + t, GU.at[l, t], z - 1 - t).wait_send()

            @pl.when((z + 1 + t < m) & ((z + 1 + t) // k != me))
            def _():
                spread_copy(l, m + t, GD.at[l, t], z + 1 + t).wait_send()

    def widen(l, d):
        f = frame(d)
        col = lax.broadcasted_iota(jnp.int32, (HW, ct), 0) % W
        for j in range(k):
            if d:
                rdma(A.at[l, f, j], A.at[l, f, j], sps.at[l, 0], ar.at[l, f, j], to(i=f)).wait_recv()
            a = A[l, f, j]
            a32 = a.astype(F32)
            left = jnp.where(col == 0, 0.0, pltpu.roll(a32, 1, 0)).astype(BF16)
            right = jnp.where(col == W - 1, 0.0, pltpu.roll(a32, HW - 1, 0)).astype(BF16)
            rows = slice(W, (H + 1) * W)
            X3[d, rows, j * ct : (j + 1) * ct] = left
            X3[d, rows, ci + j * ct : ci + (j + 1) * ct] = a
            X3[d, rows, 2 * ci + j * ct : 2 * ci + (j + 1) * ct] = right

    nt = 256 if ct % 256 == 0 else 128

    def conv(l, dx):
        @pl.loop(0, ct // nt)
        def _(b):
            cols = pl.ds(pl.multiple_of(b * nt, nt), nt)
            acc = None
            for dy in range(3):
                lhs = X3[2 * dx : 2 * dx + 2, dy * W : dy * W + HW, :].reshape(2 * HW, 3 * ci)
                part = jnp.dot(lhs, w[l, dy * 3 * ci : (dy + 1) * 3 * ci, cols], preferred_element_type=F32)
                acc = part if acc is None else acc + part
            F[dx, :, cols] = acc[:HW]
            SP[l, dx, :, cols] = acc[HW:].astype(BF16)

    def pair(l, dx):
        return rdma(SP.at[l, dx], R1.at[l, dx], s1.at[l, dx], r1.at[l, dx], to(i=frame(1)))

    def cross(l, dx):
        return rdma(SS.at[l, dx - 1], R2.at[l, dx - 1], s2.at[l, dx - 1], r2.at[l, dx - 1], to(i=frame(2 * dx)))

    def layer(l, src):
        gather(l, src)
        wcopies[l].wait()
        for dx in list(range(1, nx)) + [0]:
            widen(l, 2 * dx)
            widen(l, 2 * dx + 1)
            conv(l, dx)
            pair(l, dx).start()
            if dx:
                pair(l, dx).wait_recv()
                SS[l, dx - 1] = (F[dx] + R1[l, dx].astype(F32)).astype(BF16)
                cross(l, dx).start()
        pair(l, 0).wait_recv()
        total = F[0] + R1[l, 0].astype(F32)
        for dx in range(1, nx):
            cross(l, dx).wait_recv()
            total = total + R2[l, dx - 1].astype(F32)
        return total

    v = layer(0, x_ref)
    hid[...] = (v / (1.0 + jnp.exp(-v))).astype(BF16)
    v = layer(1, hid)
    out_ref[...] = v.astype(BF16)
    for l, src in enumerate((x_ref, hid)):
        gather_sends(l, src)
        for dx in range(nx):
            pair(l, dx).wait_send()
            if dx:
                cross(l, dx).wait_send()


def solution(mesh):
    n, m = mesh.shape["img"], mesh.shape["chan"]
    nx = n // 2

    def shards(features, kernel_one, kernel_two):
        _, H, W, ct = features.shape
        ci, co = kernel_one.shape[2:]
        HW = H * W
        k = ci // ct
        dma = pltpu.SemaphoreType.DMA
        out = pl.pallas_call(
            functools.partial(kernel, nx, m, H, W),
            out_shape=jax.ShapeDtypeStruct((HW, co), BF16),
            in_specs=[
                pl.BlockSpec(memory_space=pltpu.VMEM),
                pl.BlockSpec(memory_space=pl.ANY),
                pl.BlockSpec(memory_space=pl.ANY),
            ],
            out_specs=pl.BlockSpec(memory_space=pltpu.VMEM),
            scratch_shapes=[
                pltpu.VMEM((2, 9 * ci, co), BF16),
                pltpu.VMEM((HW, ct), BF16),
                pltpu.VMEM((2, m - 1, HW, ct), BF16),
                pltpu.VMEM((2, m - 1, HW, ct), BF16),
                pltpu.VMEM((2, n, k, HW, ct), BF16),
                pltpu.VMEM((n, (H + 2) * W, 3 * ci), BF16),
                pltpu.VMEM((nx, HW, co), F32),
                pltpu.VMEM((2, nx, HW, co), BF16),
                pltpu.VMEM((2, nx - 1, HW, co), BF16),
                pltpu.VMEM((2, nx, HW, co), BF16),
                pltpu.VMEM((2, nx - 1, HW, co), BF16),
                dma((2,)),
                dma((2, m - 1)), dma((2, m - 1)), dma((2, m - 1)), dma((2, m - 1)),
                dma((2, 2 * m - 1)), dma((2, n, k)),
                dma((2, nx)), dma((2, nx)), dma((2, nx - 1)), dma((2, nx - 1)),
            ],
            compiler_params=pltpu.CompilerParams(
                collective_id=0, has_side_effects=True, vmem_limit_bytes=56 * 1024 * 1024
            ),
        )(
            features.reshape(HW, ct),
            kernel_one.reshape(9 * ci, co),
            kernel_two.reshape(9 * ci, co),
        )
        return out.reshape(1, H, W, co)

    placed = (
        P(("groups", "img"), None, None, "chan"),
        P(None, None, "img", "chan"),
        P(None, None, "img", "chan"),
    )
    return jax.shard_map(
        shards,
        mesh=mesh,
        in_specs=placed,
        out_specs=P(("groups", "img"), None, None, "chan"),
        check_vma=False,
    )
```

```python
import functools

import jax
import jax.numpy as jnp
from jax import lax
from jax.experimental import pallas as pl
from jax.experimental.pallas import tpu as pltpu
from jax.sharding import PartitionSpec as P

MESH = pl.DeviceIdType.MESH
F32 = jnp.float32
BF16 = jnp.bfloat16
CHUNKS = 4


def kernel(
    nx, m, H, W, ins, outs,
    x_ref, k1_ref, k2_ref, out_ref,
    w, hid, GU, GD, A, X3, F, SP, SS, R1, R2,
    wsem, us, ds, ur, dr, sps, ar, s1, r1, s2, r2,
):
    n = 2 * nx
    R = len(ins[0])
    HW, ct = x_ref.shape
    ci = w.shape[1] // 9
    k = ci // ct
    me = lax.axis_index("img")
    z = lax.axis_index("chan")
    mx, core = me // 2, me % 2

    def frame(d):
        return lax.rem(mx + d // 2, nx) * 2 + (lax.rem(core + 1, 2) if d % 2 else core)

    def to(i=None, c=None):
        return {"img": me if i is None else i, "chan": z if c is None else c}

    wcopies = [pltpu.make_async_copy(kr, w.at[l], wsem.at[l]) for l, kr in enumerate((k1_ref, k2_ref))]
    for cp in wcopies:
        cp.start()

    bar = pltpu.get_barrier_semaphore()
    for d in range(1, n):
        pl.semaphore_signal(bar, inc=1, device_id=to(i=frame(d)), device_id_type=MESH)

    @pl.when(z > 0)
    def _():
        pl.semaphore_signal(bar, inc=1, device_id=to(c=z - 1), device_id_type=MESH)

    @pl.when(z < m - 1)
    def _():
        pl.semaphore_signal(bar, inc=1, device_id=to(c=z + 1), device_id_type=MESH)

    X3[:, 0:W, :] = jnp.zeros((n, W, 3 * ci), BF16)
    X3[:, (H + 1) * W : (H + 2) * W, :] = jnp.zeros((n, W, 3 * ci), BF16)
    pl.semaphore_wait(bar, n - 1 + jnp.where(z > 0, 1, 0) + jnp.where(z < m - 1, 1, 0))

    def rdma(src, dst, ss, rs, dev):
        return pltpu.make_async_remote_copy(
            src_ref=src, dst_ref=dst, send_sem=ss, recv_sem=rs, device_id=dev, device_id_type=MESH
        )

    def cut(rows):
        return pl.ds(rows[0] * W, (rows[1] - rows[0]) * W)

    def own(l, c):
        return (hid if l else x_ref).at[cut(ins[l][c])]

    def below(l, c, t):
        return GU.at[l, t, cut(ins[l][c])]

    def above(l, c, t):
        return GD.at[l, t, cut(ins[l][c])]

    def up(l, c, t):
        src = below(l, c, t - 1) if t else own(l, c)
        return rdma(src, below(l, c, t), us.at[l, c, t], ur.at[l, c, t], to(c=z + 1))

    def down(l, c, t):
        src = above(l, c, t - 1) if t else own(l, c)
        return rdma(src, above(l, c, t), ds.at[l, c, t], dr.at[l, c, t], to(c=z - 1))

    def sides(l, c):
        yield 0, own(l, c), z
        for t in range(m - 1):
            yield 1 + t, below(l, c, t), z - 1 - t
            yield m + t, above(l, c, t), z + 1 + t

    def spread_copy(l, c, q, src, s):
        return rdma(
            src, A.at[l, me, s % k, cut(ins[l][c])], sps.at[l, c, q], ar.at[l, c, me, s % k], to(i=s // k)
        )

    def spread(l, c, q, src, s):
        @pl.when(s // k != me)
        def _():
            spread_copy(l, c, q, src, s).start()

        @pl.when(s // k == me)
        def _():
            A[l, me, s % k, cut(ins[l][c])] = src[...]

    def begin_up(l, c):
        @pl.when(z < m - 1)
        def _():
            up(l, c, 0).start()

    def begin_down(l, c):
        @pl.when(z > 0)
        def _():
            down(l, c, 0).start()

    def begin(l, c):
        begin_up(l, c)
        begin_down(l, c)
        spread(l, c, 0, own(l, c), z)

    def step(l, c, t):
        more = l == 0 and c + 1 < R
        if more and t == 0:
            pl.when(z == 0)(lambda: begin_up(0, c + 1))
            pl.when(z == m - 1)(lambda: begin_down(0, c + 1))

        @pl.when(z > t)
        def _():
            up(l, c, t).wait_recv()
            if t < m - 2:
                @pl.when(z < m - 1)
                def _():
                    up(l, c, t + 1).start()
            if more:
                pl.when(z == t + 1)(lambda: begin_up(0, c + 1))
            spread(l, c, 1 + t, below(l, c, t), z - 1 - t)

        @pl.when(z + 1 + t < m)
        def _():
            down(l, c, t).wait_recv()
            if t < m - 2:
                @pl.when(z > 0)
                def _():
                    down(l, c, t + 1).start()
            if more:
                pl.when(z + 2 + t == m)(lambda: begin_down(0, c + 1))
            spread(l, c, m + t, above(l, c, t), z + 1 + t)

        if more and t == m - 2:
            spread(0, c + 1, 0, own(0, c + 1), z)

    def gather_sends(l, c):
        @pl.when(z < m - 1)
        def _():
            up(l, c, 0).wait_send()

        @pl.when(z > 0)
        def _():
            down(l, c, 0).wait_send()

        for t in range(m - 2):
            @pl.when((z > t) & (z < m - 1))
            def _():
                up(l, c, t + 1).wait_send()

            @pl.when((z + 1 + t < m) & (z > 0))
            def _():
                down(l, c, t + 1).wait_send()

        for q, src, s in sides(l, c):
            @pl.when((s >= 0) & (s < m) & (s // k != me))
            def _():
                spread_copy(l, c, q, src, s).wait_send()

    def widen(l, c, d):
        f = frame(d)
        rows = (ins[l][c][1] - ins[l][c][0]) * W
        col = lax.broadcasted_iota(jnp.int32, (rows, ct), 0) % W
        for j in range(k):
            block = A.at[l, f, j, cut(ins[l][c])]
            if d:
                rdma(block, block, sps.at[l, c, 0], ar.at[l, c, f, j], to(i=f)).wait_recv()
            a = block[...]
            a32 = a.astype(F32)
            left = jnp.where(col == 0, 0.0, pltpu.roll(a32, 1, 0)).astype(BF16)
            right = jnp.where(col == W - 1, 0.0, pltpu.roll(a32, rows - 1, 0)).astype(BF16)
            at = slice((ins[l][c][0] + 1) * W, (ins[l][c][1] + 1) * W)
            X3[d, at, j * ct : (j + 1) * ct] = left
            X3[d, at, ci + j * ct : ci + (j + 1) * ct] = a
            X3[d, at, 2 * ci + j * ct : 2 * ci + (j + 1) * ct] = right

    nt = 256 if ct % 256 == 0 else 128

    def conv(l, c):
        r0, r1 = outs[l][c]
        size = (r1 - r0) * W

        @pl.loop(0, ct // nt)
        def _(b):
            cols = pl.ds(pl.multiple_of(b * nt, nt), nt)
            acc = None
            for dy in range(3):
                lhs = X3[:, (r0 + dy) * W : (r1 + dy) * W, :].reshape(n * size, 3 * ci)
                part = jnp.dot(lhs, w[l, dy * 3 * ci : (dy + 1) * 3 * ci, cols], preferred_element_type=F32)
                acc = part if acc is None else acc + part
            for dx in range(nx):
                at = 2 * dx * size
                F[dx, cut((r0, r1)), cols] = acc[at : at + size]
                SP[l, dx, cut((r0, r1)), cols] = acc[at + size : at + 2 * size].astype(BF16)

    def pair(l, c, dx):
        at = cut(outs[l][c])
        return rdma(SP.at[l, dx, at], R1.at[l, dx, at], s1.at[l, c, dx], r1.at[l, c, dx], to(i=frame(1)))

    def cross(l, c, dx):
        at = cut(outs[l][c])
        return rdma(
            SS.at[l, dx - 1, at], R2.at[l, dx - 1, at], s2.at[l, c, dx - 1], r2.at[l, c, dx - 1], to(i=frame(2 * dx))
        )

    def finish(l, c):
        at = cut(outs[l][c])
        pair(l, c, 0).wait_recv()
        v = F[0, at] + R1[l, 0, at].astype(F32)
        for dx in range(1, nx):
            cross(l, c, dx).wait_recv()
            v = v + R2[l, dx - 1, at].astype(F32)
        if l:
            out_ref[at] = v.astype(BF16)
        else:
            hid[at] = (v / (1.0 + jnp.exp(-v))).astype(BF16)
            begin(1, c)

    units = [(l, c) for l in range(2) for c in range(R)]
    begin(0, 0)
    for t in range(m - 1):
        step(0, 0, t)
    for u, (l, c) in enumerate(units):
        later = units[u + 1] if u + 1 < len(units) else None
        if later:
            step(*later, 0)
        if c == 0:
            wcopies[l].wait()
        for d in range(n):
            widen(l, c, d)
        conv(l, c)
        for dx in list(range(1, nx)) + [0]:
            pair(l, c, dx).start()
        if later and m > 2:
            step(*later, 1)
        for dx in range(1, nx):
            pair(l, c, dx).wait_recv()
            at = cut(outs[l][c])
            SS[l, dx - 1, at] = (F[dx, at] + R1[l, dx, at].astype(F32)).astype(BF16)
            cross(l, c, dx).start()
        if later:
            for t in range(2, m - 1):
                step(*later, t)
        finish(l, c)
    for l, c in units:
        gather_sends(l, c)
        for dx in range(nx):
            pair(l, c, dx).wait_send()
            if dx:
                cross(l, c, dx).wait_send()


def solution(mesh):
    n, m = mesh.shape["img"], mesh.shape["chan"]
    nx = n // 2

    def shards(features, kernel_one, kernel_two):
        _, H, W, ct = features.shape
        ci, co = kernel_one.shape[2:]
        HW = H * W
        k = ci // ct
        tops = [H * (c + 1) // CHUNKS for c in range(CHUNKS)]
        heads = [min(t + 1, H) for t in tops]
        tails = [t - 1 for t in tops[:-1]] + [H]
        ranges = lambda ends: list(zip([0] + ends[:-1], ends))
        ins = (ranges(heads), ranges(tops))
        outs = (ranges(tops), ranges(tails))
        dma = pltpu.SemaphoreType.DMA
        out = pl.pallas_call(
            functools.partial(kernel, nx, m, H, W, ins, outs),
            out_shape=jax.ShapeDtypeStruct((HW, co), BF16),
            in_specs=[
                pl.BlockSpec(memory_space=pltpu.VMEM),
                pl.BlockSpec(memory_space=pl.ANY),
                pl.BlockSpec(memory_space=pl.ANY),
            ],
            out_specs=pl.BlockSpec(memory_space=pltpu.VMEM),
            scratch_shapes=[
                pltpu.VMEM((2, 9 * ci, co), BF16),
                pltpu.VMEM((HW, ct), BF16),
                pltpu.VMEM((2, m - 1, HW, ct), BF16),
                pltpu.VMEM((2, m - 1, HW, ct), BF16),
                pltpu.VMEM((2, n, k, HW, ct), BF16),
                pltpu.VMEM((n, (H + 2) * W, 3 * ci), BF16),
                pltpu.VMEM((nx, HW, co), F32),
                pltpu.VMEM((2, nx, HW, co), BF16),
                pltpu.VMEM((2, nx - 1, HW, co), BF16),
                pltpu.VMEM((2, nx, HW, co), BF16),
                pltpu.VMEM((2, nx - 1, HW, co), BF16),
                dma((2,)),
                dma((2, CHUNKS, m - 1)), dma((2, CHUNKS, m - 1)),
                dma((2, CHUNKS, m - 1)), dma((2, CHUNKS, m - 1)),
                dma((2, CHUNKS, 2 * m - 1)), dma((2, CHUNKS, n, k)),
                dma((2, CHUNKS, nx)), dma((2, CHUNKS, nx)),
                dma((2, CHUNKS, nx - 1)), dma((2, CHUNKS, nx - 1)),
            ],
            compiler_params=pltpu.CompilerParams(
                collective_id=0, has_side_effects=True, vmem_limit_bytes=56 * 1024 * 1024
            ),
        )(
            features.reshape(HW, ct),
            kernel_one.reshape(9 * ci, co),
            kernel_two.reshape(9 * ci, co),
        )
        return out.reshape(1, H, W, co)

    placed = (
        P(("groups", "img"), None, None, "chan"),
        P(None, None, "img", "chan"),
        P(None, None, "img", "chan"),
    )
    return jax.shard_map(
        shards,
        mesh=mesh,
        in_specs=placed,
        out_specs=P(("groups", "img"), None, None, "chan"),
        check_vma=False,
    )
```

```python
import functools

import jax
import jax.numpy as jnp
from jax import lax
from jax.experimental import pallas as pl
from jax.experimental.pallas import tpu as pltpu
from jax.sharding import PartitionSpec as P

MESH = pl.DeviceIdType.MESH
F32 = jnp.float32
BF16 = jnp.bfloat16
CHUNKS = 4


def kernel(
    nx, m, H, W, ins, outs,
    x_ref, k1_ref, k2_ref, out_ref,
    w, hid, GU, GD, A, X3, F, SP, SS, R1, R2,
    wsem, us, ds, ur, dr, sps, ar, s1, r1, s2, r2,
):
    n = 2 * nx
    R = len(ins[0])
    HW, ct = x_ref.shape
    ci = w.shape[1] // 9
    k = ci // ct
    me = lax.axis_index("img")
    z = lax.axis_index("chan")
    mx, core = me // 2, me % 2

    def frame(d):
        return lax.rem(mx + d // 2, nx) * 2 + (lax.rem(core + 1, 2) if d % 2 else core)

    def to(i=None, c=None):
        return {"img": me if i is None else i, "chan": z if c is None else c}

    wcopies = [pltpu.make_async_copy(kr, w.at[l], wsem.at[l]) for l, kr in enumerate((k1_ref, k2_ref))]
    for cp in wcopies:
        cp.start()

    bar = pltpu.get_barrier_semaphore()
    for d in range(1, n):
        pl.semaphore_signal(bar, inc=1, device_id=to(i=frame(d)), device_id_type=MESH)

    @pl.when(z > 0)
    def _():
        pl.semaphore_signal(bar, inc=1, device_id=to(c=z - 1), device_id_type=MESH)

    @pl.when(z < m - 1)
    def _():
        pl.semaphore_signal(bar, inc=1, device_id=to(c=z + 1), device_id_type=MESH)

    X3[:, 0:W, :] = jnp.zeros((n, W, 3 * ci), BF16)
    X3[:, (H + 1) * W : (H + 2) * W, :] = jnp.zeros((n, W, 3 * ci), BF16)
    pl.semaphore_wait(bar, n - 1 + jnp.where(z > 0, 1, 0) + jnp.where(z < m - 1, 1, 0))

    def rdma(src, dst, ss, rs, dev):
        return pltpu.make_async_remote_copy(
            src_ref=src, dst_ref=dst, send_sem=ss, recv_sem=rs, device_id=dev, device_id_type=MESH
        )

    def cut(rows):
        return pl.ds(rows[0] * W, (rows[1] - rows[0]) * W)

    def own(l, c):
        return (hid if l else x_ref).at[cut(ins[l][c])]

    def below(l, c, t):
        return GU.at[l, t, cut(ins[l][c])]

    def above(l, c, t):
        return GD.at[l, t, cut(ins[l][c])]

    def up(l, c, t):
        src = below(l, c, t - 1) if t else own(l, c)
        return rdma(src, below(l, c, t), us.at[l, c, t], ur.at[l, c, t], to(c=z + 1))

    def down(l, c, t):
        src = above(l, c, t - 1) if t else own(l, c)
        return rdma(src, above(l, c, t), ds.at[l, c, t], dr.at[l, c, t], to(c=z - 1))

    def sides(l, c):
        yield 0, own(l, c), z
        for t in range(m - 1):
            yield 1 + t, below(l, c, t), z - 1 - t
            yield m + t, above(l, c, t), z + 1 + t

    def spread_copy(l, c, q, src, s):
        return rdma(
            src, A.at[l, me, s % k, cut(ins[l][c])], sps.at[l, c, q], ar.at[l, c, me, s % k], to(i=s // k)
        )

    def spread(l, c, q, src, s):
        @pl.when(s // k != me)
        def _():
            spread_copy(l, c, q, src, s).start()

        @pl.when(s // k == me)
        def _():
            A[l, me, s % k, cut(ins[l][c])] = src[...]

    def begin_up(l, c):
        @pl.when(z < m - 1)
        def _():
            up(l, c, 0).start()

    def begin_down(l, c):
        @pl.when(z > 0)
        def _():
            down(l, c, 0).start()

    def begin(l, c):
        begin_up(l, c)
        begin_down(l, c)
        spread(l, c, 0, own(l, c), z)

    def step(l, c, t):
        more = l == 0 and c + 2 < R
        if more and t == 0:
            pl.when(z == 0)(lambda: begin_up(0, c + 2))
            pl.when(z == m - 1)(lambda: begin_down(0, c + 2))

        @pl.when(z > t)
        def _():
            up(l, c, t).wait_recv()
            if t < m - 2:
                @pl.when(z < m - 1)
                def _():
                    up(l, c, t + 1).start()
            if more:
                pl.when(z == t + 1)(lambda: begin_up(0, c + 2))
            spread(l, c, 1 + t, below(l, c, t), z - 1 - t)

        @pl.when(z + 1 + t < m)
        def _():
            down(l, c, t).wait_recv()
            if t < m - 2:
                @pl.when(z > 0)
                def _():
                    down(l, c, t + 1).start()
            if more:
                pl.when(z + 2 + t == m)(lambda: begin_down(0, c + 2))
            spread(l, c, m + t, above(l, c, t), z + 1 + t)

        if more and t == m - 2:
            spread(0, c + 2, 0, own(0, c + 2), z)

    def gather_sends(l, c):
        @pl.when(z < m - 1)
        def _():
            up(l, c, 0).wait_send()

        @pl.when(z > 0)
        def _():
            down(l, c, 0).wait_send()

        for t in range(m - 2):
            @pl.when((z > t) & (z < m - 1))
            def _():
                up(l, c, t + 1).wait_send()

            @pl.when((z + 1 + t < m) & (z > 0))
            def _():
                down(l, c, t + 1).wait_send()

        for q, src, s in sides(l, c):
            @pl.when((s >= 0) & (s < m) & (s // k != me))
            def _():
                spread_copy(l, c, q, src, s).wait_send()

    def widen(l, c, d):
        f = frame(d)
        rows = (ins[l][c][1] - ins[l][c][0]) * W
        col = lax.broadcasted_iota(jnp.int32, (rows, ct), 0) % W
        for j in range(k):
            block = A.at[l, f, j, cut(ins[l][c])]
            if d:
                rdma(block, block, sps.at[l, c, 0], ar.at[l, c, f, j], to(i=f)).wait_recv()
            a = block[...]
            a32 = a.astype(F32)
            left = jnp.where(col == 0, 0.0, pltpu.roll(a32, 1, 0)).astype(BF16)
            right = jnp.where(col == W - 1, 0.0, pltpu.roll(a32, rows - 1, 0)).astype(BF16)
            at = slice((ins[l][c][0] + 1) * W, (ins[l][c][1] + 1) * W)
            X3[d, at, j * ct : (j + 1) * ct] = left
            X3[d, at, ci + j * ct : ci + (j + 1) * ct] = a
            X3[d, at, 2 * ci + j * ct : 2 * ci + (j + 1) * ct] = right

    nt = 256 if ct % 256 == 0 else 128

    def conv(l, c):
        r0, r1 = outs[l][c]
        size = (r1 - r0) * W

        @pl.loop(0, ct // nt)
        def _(b):
            cols = pl.ds(pl.multiple_of(b * nt, nt), nt)
            acc = None
            for dy in range(3):
                lhs = X3[:, (r0 + dy) * W : (r1 + dy) * W, :].reshape(n * size, 3 * ci)
                part = jnp.dot(lhs, w[l, dy * 3 * ci : (dy + 1) * 3 * ci, cols], preferred_element_type=F32)
                acc = part if acc is None else acc + part
            for dx in range(nx):
                at = 2 * dx * size
                F[dx, cut((r0, r1)), cols] = acc[at : at + size]
                SP[l, dx, cut((r0, r1)), cols] = acc[at + size : at + 2 * size].astype(BF16)

    def pair(l, c, dx):
        at = cut(outs[l][c])
        return rdma(SP.at[l, dx, at], R1.at[l, dx, at], s1.at[l, c, dx], r1.at[l, c, dx], to(i=frame(1)))

    def cross(l, c, dx):
        at = cut(outs[l][c])
        return rdma(
            SS.at[l, dx - 1, at], R2.at[l, dx - 1, at], s2.at[l, c, dx - 1], r2.at[l, c, dx - 1], to(i=frame(2 * dx))
        )

    def finish(l, c):
        at = cut(outs[l][c])
        pair(l, c, 0).wait_recv()
        v = F[0, at] + R1[l, 0, at].astype(F32)
        for dx in range(1, nx):
            cross(l, c, dx).wait_recv()
            v = v + R2[l, dx - 1, at].astype(F32)
        if l:
            out_ref[at] = v.astype(BF16)
        else:
            hid[at] = (v / (1.0 + jnp.exp(-v))).astype(BF16)
            begin(1, c)

    units = [(l, c) for l in range(2) for c in range(R)]
    begin(0, 0)
    begin(0, 1)
    for t in range(m - 1):
        step(0, 0, t)
    for u, (l, c) in enumerate(units):
        later = units[u + 1] if u + 1 < len(units) else None
        if later:
            step(*later, 0)
        if c == 0:
            wcopies[l].wait()
        for d in range(n):
            widen(l, c, d)
        conv(l, c)
        for dx in list(range(1, nx)) + [0]:
            pair(l, c, dx).start()
        if u:
            finish(*units[u - 1])
        if later and m > 2:
            step(*later, 1)
        for dx in range(1, nx):
            pair(l, c, dx).wait_recv()
            at = cut(outs[l][c])
            SS[l, dx - 1, at] = (F[dx, at] + R1[l, dx, at].astype(F32)).astype(BF16)
            cross(l, c, dx).start()
        if later:
            for t in range(2, m - 1):
                step(*later, t)
    finish(*units[-1])
    for l, c in units:
        gather_sends(l, c)
        for dx in range(nx):
            pair(l, c, dx).wait_send()
            if dx:
                cross(l, c, dx).wait_send()


def solution(mesh):
    n, m = mesh.shape["img"], mesh.shape["chan"]
    nx = n // 2

    def shards(features, kernel_one, kernel_two):
        _, H, W, ct = features.shape
        ci, co = kernel_one.shape[2:]
        HW = H * W
        k = ci // ct
        tops = [H * (c + 1) // CHUNKS for c in range(CHUNKS)]
        heads = [min(t + 1, H) for t in tops]
        tails = [t - 1 for t in tops[:-1]] + [H]
        ranges = lambda ends: list(zip([0] + ends[:-1], ends))
        ins = (ranges(heads), ranges(tops))
        outs = (ranges(tops), ranges(tails))
        dma = pltpu.SemaphoreType.DMA
        out = pl.pallas_call(
            functools.partial(kernel, nx, m, H, W, ins, outs),
            out_shape=jax.ShapeDtypeStruct((HW, co), BF16),
            in_specs=[
                pl.BlockSpec(memory_space=pltpu.VMEM),
                pl.BlockSpec(memory_space=pl.ANY),
                pl.BlockSpec(memory_space=pl.ANY),
            ],
            out_specs=pl.BlockSpec(memory_space=pltpu.VMEM),
            scratch_shapes=[
                pltpu.VMEM((2, 9 * ci, co), BF16),
                pltpu.VMEM((HW, ct), BF16),
                pltpu.VMEM((2, m - 1, HW, ct), BF16),
                pltpu.VMEM((2, m - 1, HW, ct), BF16),
                pltpu.VMEM((2, n, k, HW, ct), BF16),
                pltpu.VMEM((n, (H + 2) * W, 3 * ci), BF16),
                pltpu.VMEM((nx, HW, co), F32),
                pltpu.VMEM((2, nx, HW, co), BF16),
                pltpu.VMEM((2, nx - 1, HW, co), BF16),
                pltpu.VMEM((2, nx, HW, co), BF16),
                pltpu.VMEM((2, nx - 1, HW, co), BF16),
                dma((2,)),
                dma((2, CHUNKS, m - 1)), dma((2, CHUNKS, m - 1)),
                dma((2, CHUNKS, m - 1)), dma((2, CHUNKS, m - 1)),
                dma((2, CHUNKS, 2 * m - 1)), dma((2, CHUNKS, n, k)),
                dma((2, CHUNKS, nx)), dma((2, CHUNKS, nx)),
                dma((2, CHUNKS, nx - 1)), dma((2, CHUNKS, nx - 1)),
            ],
            compiler_params=pltpu.CompilerParams(
                collective_id=0, has_side_effects=True, vmem_limit_bytes=56 * 1024 * 1024
            ),
        )(
            features.reshape(HW, ct),
            kernel_one.reshape(9 * ci, co),
            kernel_two.reshape(9 * ci, co),
        )
        return out.reshape(1, H, W, co)

    placed = (
        P(("groups", "img"), None, None, "chan"),
        P(None, None, "img", "chan"),
        P(None, None, "img", "chan"),
    )
    return jax.shard_map(
        shards,
        mesh=mesh,
        in_specs=placed,
        out_specs=P(("groups", "img"), None, None, "chan"),
        check_vma=False,
    )
```

```python
import functools

import jax
import jax.numpy as jnp
from jax import lax
from jax.experimental import pallas as pl
from jax.experimental.pallas import tpu as pltpu
from jax.sharding import PartitionSpec as P

MESH = pl.DeviceIdType.MESH
F32 = jnp.float32
BF16 = jnp.bfloat16
CHUNKS = 4


def kernel(
    nx, m, H, W, ins, outs,
    x_ref, k1_ref, k2_ref, out_ref,
    w, hid, GU, GD, A, X3, F, SP, SS, R1, R2,
    wsem, us, ds, ur, dr, sps, ar, s1, r1, s2, r2,
):
    n = 2 * nx
    R = len(ins[0])
    HW, ct = x_ref.shape
    ci = w.shape[1] // 9
    k = ci // ct
    me = lax.axis_index("img")
    z = lax.axis_index("chan")
    mx, core = me // 2, me % 2

    def frame(d):
        return lax.rem(mx + d // 2, nx) * 2 + (lax.rem(core + 1, 2) if d % 2 else core)

    def to(i=None, c=None):
        return {"img": me if i is None else i, "chan": z if c is None else c}

    wcopies = [pltpu.make_async_copy(kr, w.at[l], wsem.at[l]) for l, kr in enumerate((k1_ref, k2_ref))]
    for cp in wcopies:
        cp.start()

    bar = pltpu.get_barrier_semaphore()
    for d in range(1, n):
        pl.semaphore_signal(bar, inc=1, device_id=to(i=frame(d)), device_id_type=MESH)

    @pl.when(z > 0)
    def _():
        pl.semaphore_signal(bar, inc=1, device_id=to(c=z - 1), device_id_type=MESH)

    @pl.when(z < m - 1)
    def _():
        pl.semaphore_signal(bar, inc=1, device_id=to(c=z + 1), device_id_type=MESH)

    X3[:, 0:W, :] = jnp.zeros((n, W, 3 * ci), BF16)
    X3[:, (H + 1) * W : (H + 2) * W, :] = jnp.zeros((n, W, 3 * ci), BF16)
    pl.semaphore_wait(bar, n - 1 + jnp.where(z > 0, 1, 0) + jnp.where(z < m - 1, 1, 0))

    def rdma(src, dst, ss, rs, dev):
        return pltpu.make_async_remote_copy(
            src_ref=src, dst_ref=dst, send_sem=ss, recv_sem=rs, device_id=dev, device_id_type=MESH
        )

    def cut(rows):
        return pl.ds(rows[0] * W, (rows[1] - rows[0]) * W)

    def own(l, c):
        return (hid if l else x_ref).at[cut(ins[l][c])]

    def below(l, c, t):
        return GU.at[l, t, cut(ins[l][c])]

    def above(l, c, t):
        return GD.at[l, t, cut(ins[l][c])]

    def up(l, c, t):
        src = below(l, c, t - 1) if t else own(l, c)
        return rdma(src, below(l, c, t), us.at[l, c, t], ur.at[l, c, t], to(c=z + 1))

    def down(l, c, t):
        src = above(l, c, t - 1) if t else own(l, c)
        return rdma(src, above(l, c, t), ds.at[l, c, t], dr.at[l, c, t], to(c=z - 1))

    def sides(l, c):
        yield 0, own(l, c), z
        for t in range(m - 1):
            yield 1 + t, below(l, c, t), z - 1 - t
            yield m + t, above(l, c, t), z + 1 + t

    def spread_copy(l, c, q, src, s):
        return rdma(
            src, A.at[l, me, s % k, cut(ins[l][c])], sps.at[l, c, q], ar.at[l, c, me, s % k], to(i=s // k)
        )

    def spread(l, c, q, src, s):
        @pl.when(s // k != me)
        def _():
            spread_copy(l, c, q, src, s).start()

        @pl.when(s // k == me)
        def _():
            A[l, me, s % k, cut(ins[l][c])] = src[...]

    def begin_up(l, c):
        @pl.when(z < m - 1)
        def _():
            up(l, c, 0).start()

    def begin_down(l, c):
        @pl.when(z > 0)
        def _():
            down(l, c, 0).start()

    def begin(l, c):
        begin_up(l, c)
        begin_down(l, c)
        spread(l, c, 0, own(l, c), z)

    def step(l, c, t):
        more = l == 0 and c + 2 < R
        if more and t == 0:
            pl.when(z == 0)(lambda: begin_up(0, c + 2))
            pl.when(z == m - 1)(lambda: begin_down(0, c + 2))

        @pl.when(z > t)
        def _():
            up(l, c, t).wait_recv()
            if t < m - 2:
                @pl.when(z < m - 1)
                def _():
                    up(l, c, t + 1).start()
            if more:
                pl.when(z == t + 1)(lambda: begin_up(0, c + 2))
            spread(l, c, 1 + t, below(l, c, t), z - 1 - t)

        @pl.when(z + 1 + t < m)
        def _():
            down(l, c, t).wait_recv()
            if t < m - 2:
                @pl.when(z > 0)
                def _():
                    down(l, c, t + 1).start()
            if more:
                pl.when(z + 2 + t == m)(lambda: begin_down(0, c + 2))
            spread(l, c, m + t, above(l, c, t), z + 1 + t)

        if more and t == m - 2:
            spread(0, c + 2, 0, own(0, c + 2), z)

    def gather_sends(l, c):
        @pl.when(z < m - 1)
        def _():
            up(l, c, 0).wait_send()

        @pl.when(z > 0)
        def _():
            down(l, c, 0).wait_send()

        for t in range(m - 2):
            @pl.when((z > t) & (z < m - 1))
            def _():
                up(l, c, t + 1).wait_send()

            @pl.when((z + 1 + t < m) & (z > 0))
            def _():
                down(l, c, t + 1).wait_send()

        for q, src, s in sides(l, c):
            @pl.when((s >= 0) & (s < m) & (s // k != me))
            def _():
                spread_copy(l, c, q, src, s).wait_send()

    def widen(l, c, d):
        f = frame(d)
        rows = (ins[l][c][1] - ins[l][c][0]) * W
        col = lax.broadcasted_iota(jnp.int32, (rows, ct), 0) % W
        for j in range(k):
            block = A.at[l, f, j, cut(ins[l][c])]
            if d:
                rdma(block, block, sps.at[l, c, 0], ar.at[l, c, f, j], to(i=f)).wait_recv()
            a = block[...]
            a32 = a.astype(F32)
            left = jnp.where(col == 0, 0.0, pltpu.roll(a32, 1, 0)).astype(BF16)
            right = jnp.where(col == W - 1, 0.0, pltpu.roll(a32, rows - 1, 0)).astype(BF16)
            at = slice((ins[l][c][0] + 1) * W, (ins[l][c][1] + 1) * W)
            X3[d, at, j * ct : (j + 1) * ct] = left
            X3[d, at, ci + j * ct : ci + (j + 1) * ct] = a
            X3[d, at, 2 * ci + j * ct : 2 * ci + (j + 1) * ct] = right

    nt = 256 if ct % 256 == 0 else 128

    def conv(l, c):
        r0, r1 = outs[l][c]
        size = (r1 - r0) * W

        @pl.loop(0, ct // nt)
        def _(b):
            cols = pl.ds(pl.multiple_of(b * nt, nt), nt)
            acc = None
            for dy in range(3):
                lhs = X3[:, (r0 + dy) * W : (r1 + dy) * W, :].reshape(n * size, 3 * ci)
                part = jnp.dot(lhs, w[l, dy * 3 * ci : (dy + 1) * 3 * ci, cols], preferred_element_type=F32)
                acc = part if acc is None else acc + part
            for dx in range(nx):
                at = 2 * dx * size
                F[dx, cut((r0, r1)), cols] = acc[at : at + size]
                SP[l, dx, cut((r0, r1)), cols] = acc[at + size : at + 2 * size].astype(BF16)

    def pair(l, c, dx):
        at = cut(outs[l][c])
        return rdma(SP.at[l, dx, at], R1.at[l, dx, at], s1.at[l, c, dx], r1.at[l, c, dx], to(i=frame(1)))

    def cross(l, c, dx):
        at = cut(outs[l][c])
        return rdma(
            SS.at[l, dx - 1, at], R2.at[l, dx - 1, at], s2.at[l, c, dx - 1], r2.at[l, c, dx - 1], to(i=frame(2 * dx))
        )

    def finish(l, c):
        at = cut(outs[l][c])
        pair(l, c, 0).wait_recv()
        v = F[0, at] + R1[l, 0, at].astype(F32)
        for dx in range(1, nx):
            cross(l, c, dx).wait_recv()
            v = v + R2[l, dx - 1, at].astype(F32)
        if l:
            out_ref[at] = v.astype(BF16)
        else:
            hid[at] = (v / (1.0 + jnp.exp(-v))).astype(BF16)
            begin(1, c)

    units = [(l, c) for l in range(2) for c in range(R)]
    begin(0, 0)
    begin(0, 1)
    last = m - 2

    def ahead(i, first, stop):
        if i < len(units):
            for t in range(first, stop):
                step(*units[i], t)

    ahead(0, 0, m - 1)
    ahead(1, 0, last)
    for u, (l, c) in enumerate(units):
        if c == 0:
            wcopies[l].wait()
        for d in range(n):
            widen(l, c, d)
        conv(l, c)
        for dx in list(range(1, nx)) + [0]:
            pair(l, c, dx).start()
        ahead(u + 2, 0, min(1, last))
        ahead(u + 1, last, m - 1)
        for dx in range(1, nx):
            pair(l, c, dx).wait_recv()
            at = cut(outs[l][c])
            SS[l, dx - 1, at] = (F[dx, at] + R1[l, dx, at].astype(F32)).astype(BF16)
            cross(l, c, dx).start()
        if u:
            finish(*units[u - 1])
        ahead(u + 2, 1, last)
    finish(*units[-1])
    for l, c in units:
        gather_sends(l, c)
        for dx in range(nx):
            pair(l, c, dx).wait_send()
            if dx:
                cross(l, c, dx).wait_send()


def solution(mesh):
    n, m = mesh.shape["img"], mesh.shape["chan"]
    nx = n // 2

    def shards(features, kernel_one, kernel_two):
        _, H, W, ct = features.shape
        ci, co = kernel_one.shape[2:]
        HW = H * W
        k = ci // ct
        tops = [H * (c + 1) // CHUNKS for c in range(CHUNKS)]
        heads = [min(t + 1, H) for t in tops]
        tails = [t - 1 for t in tops[:-1]] + [H]
        ranges = lambda ends: list(zip([0] + ends[:-1], ends))
        ins = (ranges(heads), ranges(tops))
        outs = (ranges(tops), ranges(tails))
        dma = pltpu.SemaphoreType.DMA
        out = pl.pallas_call(
            functools.partial(kernel, nx, m, H, W, ins, outs),
            out_shape=jax.ShapeDtypeStruct((HW, co), BF16),
            in_specs=[
                pl.BlockSpec(memory_space=pltpu.VMEM),
                pl.BlockSpec(memory_space=pl.ANY),
                pl.BlockSpec(memory_space=pl.ANY),
            ],
            out_specs=pl.BlockSpec(memory_space=pltpu.VMEM),
            scratch_shapes=[
                pltpu.VMEM((2, 9 * ci, co), BF16),
                pltpu.VMEM((HW, ct), BF16),
                pltpu.VMEM((2, m - 1, HW, ct), BF16),
                pltpu.VMEM((2, m - 1, HW, ct), BF16),
                pltpu.VMEM((2, n, k, HW, ct), BF16),
                pltpu.VMEM((n, (H + 2) * W, 3 * ci), BF16),
                pltpu.VMEM((nx, HW, co), F32),
                pltpu.VMEM((2, nx, HW, co), BF16),
                pltpu.VMEM((2, nx - 1, HW, co), BF16),
                pltpu.VMEM((2, nx, HW, co), BF16),
                pltpu.VMEM((2, nx - 1, HW, co), BF16),
                dma((2,)),
                dma((2, CHUNKS, m - 1)), dma((2, CHUNKS, m - 1)),
                dma((2, CHUNKS, m - 1)), dma((2, CHUNKS, m - 1)),
                dma((2, CHUNKS, 2 * m - 1)), dma((2, CHUNKS, n, k)),
                dma((2, CHUNKS, nx)), dma((2, CHUNKS, nx)),
                dma((2, CHUNKS, nx - 1)), dma((2, CHUNKS, nx - 1)),
            ],
            compiler_params=pltpu.CompilerParams(
                collective_id=0, has_side_effects=True, vmem_limit_bytes=56 * 1024 * 1024
            ),
        )(
            features.reshape(HW, ct),
            kernel_one.reshape(9 * ci, co),
            kernel_two.reshape(9 * ci, co),
        )
        return out.reshape(1, H, W, co)

    placed = (
        P(("groups", "img"), None, None, "chan"),
        P(None, None, "img", "chan"),
        P(None, None, "img", "chan"),
    )
    return jax.shard_map(
        shards,
        mesh=mesh,
        in_specs=placed,
        out_specs=P(("groups", "img"), None, None, "chan"),
        check_vma=False,
    )
```

```python
import functools

import jax
import jax.numpy as jnp
from jax import lax
from jax.experimental import pallas as pl
from jax.experimental.pallas import tpu as pltpu
from jax.sharding import PartitionSpec as P

MESH = pl.DeviceIdType.MESH
F32 = jnp.float32
BF16 = jnp.bfloat16
CHUNKS = 5


def kernel(
    nx, m, H, W, ins, outs,
    x_ref, k1_ref, k2_ref, out_ref,
    w, hid, GU, GD, A, X3, F, SP, SS, R1, R2,
    wsem, us, ds, ur, dr, sps, ar, s1, r1, s2, r2,
):
    n = 2 * nx
    R = len(ins[0])
    HW, ct = x_ref.shape
    ci = w.shape[1] // 9
    k = ci // ct
    me = lax.axis_index("img")
    z = lax.axis_index("chan")
    mx, core = me // 2, me % 2

    def frame(d):
        return lax.rem(mx + d // 2, nx) * 2 + (lax.rem(core + 1, 2) if d % 2 else core)

    def to(i=None, c=None):
        return {"img": me if i is None else i, "chan": z if c is None else c}

    wcopies = [pltpu.make_async_copy(kr, w.at[l], wsem.at[l]) for l, kr in enumerate((k1_ref, k2_ref))]
    for cp in wcopies:
        cp.start()

    bar = pltpu.get_barrier_semaphore()
    for d in range(1, n):
        pl.semaphore_signal(bar, inc=1, device_id=to(i=frame(d)), device_id_type=MESH)

    @pl.when(z > 0)
    def _():
        pl.semaphore_signal(bar, inc=1, device_id=to(c=z - 1), device_id_type=MESH)

    @pl.when(z < m - 1)
    def _():
        pl.semaphore_signal(bar, inc=1, device_id=to(c=z + 1), device_id_type=MESH)

    X3[:, 0:W, :] = jnp.zeros((n, W, 3 * ci), BF16)
    X3[:, (H + 1) * W : (H + 2) * W, :] = jnp.zeros((n, W, 3 * ci), BF16)
    pl.semaphore_wait(bar, n - 1 + jnp.where(z > 0, 1, 0) + jnp.where(z < m - 1, 1, 0))

    def rdma(src, dst, ss, rs, dev):
        return pltpu.make_async_remote_copy(
            src_ref=src, dst_ref=dst, send_sem=ss, recv_sem=rs, device_id=dev, device_id_type=MESH
        )

    def cut(rows):
        return pl.ds(rows[0] * W, (rows[1] - rows[0]) * W)

    def own(l, c):
        return (hid if l else x_ref).at[cut(ins[l][c])]

    def below(l, c, t):
        return GU.at[l, t, cut(ins[l][c])]

    def above(l, c, t):
        return GD.at[l, t, cut(ins[l][c])]

    def up(l, c, t):
        src = below(l, c, t - 1) if t else own(l, c)
        return rdma(src, below(l, c, t), us.at[l, c, t], ur.at[l, c, t], to(c=z + 1))

    def down(l, c, t):
        src = above(l, c, t - 1) if t else own(l, c)
        return rdma(src, above(l, c, t), ds.at[l, c, t], dr.at[l, c, t], to(c=z - 1))

    def sides(l, c):
        yield 0, own(l, c), z
        for t in range(m - 1):
            yield 1 + t, below(l, c, t), z - 1 - t
            yield m + t, above(l, c, t), z + 1 + t

    def spread_copy(l, c, q, src, s):
        return rdma(
            src, A.at[l, me, s % k, cut(ins[l][c])], sps.at[l, c, q], ar.at[l, c, me, s % k], to(i=s // k)
        )

    def spread(l, c, q, src, s):
        @pl.when(s // k != me)
        def _():
            spread_copy(l, c, q, src, s).start()

        @pl.when(s // k == me)
        def _():
            A[l, me, s % k, cut(ins[l][c])] = src[...]

    def begin_up(l, c):
        @pl.when(z < m - 1)
        def _():
            up(l, c, 0).start()

    def begin_down(l, c):
        @pl.when(z > 0)
        def _():
            down(l, c, 0).start()

    def begin(l, c):
        begin_up(l, c)
        begin_down(l, c)
        spread(l, c, 0, own(l, c), z)

    def step(l, c, t):
        more = l == 0 and c + 2 < R
        if more and t == 0:
            pl.when(z == 0)(lambda: begin_up(0, c + 2))
            pl.when(z == m - 1)(lambda: begin_down(0, c + 2))

        @pl.when(z > t)
        def _():
            up(l, c, t).wait_recv()
            if t < m - 2:
                @pl.when(z < m - 1)
                def _():
                    up(l, c, t + 1).start()
            if more:
                pl.when(z == t + 1)(lambda: begin_up(0, c + 2))
            spread(l, c, 1 + t, below(l, c, t), z - 1 - t)

        @pl.when(z + 1 + t < m)
        def _():
            down(l, c, t).wait_recv()
            if t < m - 2:
                @pl.when(z > 0)
                def _():
                    down(l, c, t + 1).start()
            if more:
                pl.when(z + 2 + t == m)(lambda: begin_down(0, c + 2))
            spread(l, c, m + t, above(l, c, t), z + 1 + t)

        if more and t == m - 2:
            spread(0, c + 2, 0, own(0, c + 2), z)

    def gather_sends(l, c):
        @pl.when(z < m - 1)
        def _():
            up(l, c, 0).wait_send()

        @pl.when(z > 0)
        def _():
            down(l, c, 0).wait_send()

        for t in range(m - 2):
            @pl.when((z > t) & (z < m - 1))
            def _():
                up(l, c, t + 1).wait_send()

            @pl.when((z + 1 + t < m) & (z > 0))
            def _():
                down(l, c, t + 1).wait_send()

        for q, src, s in sides(l, c):
            @pl.when((s >= 0) & (s < m) & (s // k != me))
            def _():
                spread_copy(l, c, q, src, s).wait_send()

    def widen(l, c, d):
        f = frame(d)
        rows = (ins[l][c][1] - ins[l][c][0]) * W
        col = lax.broadcasted_iota(jnp.int32, (rows, ct), 0) % W
        for j in range(k):
            block = A.at[l, f, j, cut(ins[l][c])]
            if d:
                rdma(block, block, sps.at[l, c, 0], ar.at[l, c, f, j], to(i=f)).wait_recv()
            a = block[...]
            a32 = a.astype(F32)
            left = jnp.where(col == 0, 0.0, pltpu.roll(a32, 1, 0)).astype(BF16)
            right = jnp.where(col == W - 1, 0.0, pltpu.roll(a32, rows - 1, 0)).astype(BF16)
            at = slice((ins[l][c][0] + 1) * W, (ins[l][c][1] + 1) * W)
            X3[d, at, j * ct : (j + 1) * ct] = left
            X3[d, at, ci + j * ct : ci + (j + 1) * ct] = a
            X3[d, at, 2 * ci + j * ct : 2 * ci + (j + 1) * ct] = right

    nt = 256 if ct % 256 == 0 else 128

    def conv(l, c):
        r0, r1 = outs[l][c]
        size = (r1 - r0) * W

        @pl.loop(0, ct // nt)
        def _(b):
            cols = pl.ds(pl.multiple_of(b * nt, nt), nt)
            acc = None
            for dy in range(3):
                lhs = X3[:, (r0 + dy) * W : (r1 + dy) * W, :].reshape(n * size, 3 * ci)
                part = jnp.dot(lhs, w[l, dy * 3 * ci : (dy + 1) * 3 * ci, cols], preferred_element_type=F32)
                acc = part if acc is None else acc + part
            for dx in range(nx):
                at = 2 * dx * size
                F[dx, cut((r0, r1)), cols] = acc[at : at + size]
                SP[l, dx, cut((r0, r1)), cols] = acc[at + size : at + 2 * size].astype(BF16)

    def pair(l, c, dx):
        at = cut(outs[l][c])
        return rdma(SP.at[l, dx, at], R1.at[l, dx, at], s1.at[l, c, dx], r1.at[l, c, dx], to(i=frame(1)))

    def cross(l, c, dx):
        at = cut(outs[l][c])
        return rdma(
            SS.at[l, dx - 1, at], R2.at[l, dx - 1, at], s2.at[l, c, dx - 1], r2.at[l, c, dx - 1], to(i=frame(2 * dx))
        )

    def finish(l, c):
        at = cut(outs[l][c])
        pair(l, c, 0).wait_recv()
        v = F[0, at] + R1[l, 0, at].astype(F32)
        for dx in range(1, nx):
            cross(l, c, dx).wait_recv()
            v = v + R2[l, dx - 1, at].astype(F32)
        if l:
            out_ref[at] = v.astype(BF16)
        else:
            hid[at] = (v / (1.0 + jnp.exp(-v))).astype(BF16)
            begin(1, c)

    units = [(l, c) for l in range(2) for c in range(R)]
    begin(0, 0)
    begin(0, 1)
    last = m - 2

    def ahead(i, first, stop):
        if i < len(units):
            for t in range(first, stop):
                step(*units[i], t)

    ahead(0, 0, m - 1)
    ahead(1, 0, last)
    for u, (l, c) in enumerate(units):
        if c == 0:
            wcopies[l].wait()
        for d in range(n):
            widen(l, c, d)
        conv(l, c)
        for dx in list(range(1, nx)) + [0]:
            pair(l, c, dx).start()
        ahead(u + 2, 0, min(1, last))
        ahead(u + 1, last, m - 1)
        for dx in range(1, nx):
            pair(l, c, dx).wait_recv()
            at = cut(outs[l][c])
            SS[l, dx - 1, at] = (F[dx, at] + R1[l, dx, at].astype(F32)).astype(BF16)
            cross(l, c, dx).start()
        if u:
            finish(*units[u - 1])
        ahead(u + 2, 1, last)
    finish(*units[-1])
    for l, c in units:
        gather_sends(l, c)
        for dx in range(nx):
            pair(l, c, dx).wait_send()
            if dx:
                cross(l, c, dx).wait_send()


def solution(mesh):
    n, m = mesh.shape["img"], mesh.shape["chan"]
    nx = n // 2

    def shards(features, kernel_one, kernel_two):
        _, H, W, ct = features.shape
        ci, co = kernel_one.shape[2:]
        HW = H * W
        k = ci // ct
        tops = [H * (c + 1) // CHUNKS for c in range(CHUNKS)]
        heads = [min(t + 1, H) for t in tops]
        tails = [t - 1 for t in tops[:-1]] + [H]
        ranges = lambda ends: list(zip([0] + ends[:-1], ends))
        ins = (ranges(heads), ranges(tops))
        outs = (ranges(tops), ranges(tails))
        dma = pltpu.SemaphoreType.DMA
        out = pl.pallas_call(
            functools.partial(kernel, nx, m, H, W, ins, outs),
            out_shape=jax.ShapeDtypeStruct((HW, co), BF16),
            in_specs=[
                pl.BlockSpec(memory_space=pltpu.VMEM),
                pl.BlockSpec(memory_space=pl.ANY),
                pl.BlockSpec(memory_space=pl.ANY),
            ],
            out_specs=pl.BlockSpec(memory_space=pltpu.VMEM),
            scratch_shapes=[
                pltpu.VMEM((2, 9 * ci, co), BF16),
                pltpu.VMEM((HW, ct), BF16),
                pltpu.VMEM((2, m - 1, HW, ct), BF16),
                pltpu.VMEM((2, m - 1, HW, ct), BF16),
                pltpu.VMEM((2, n, k, HW, ct), BF16),
                pltpu.VMEM((n, (H + 2) * W, 3 * ci), BF16),
                pltpu.VMEM((nx, HW, co), F32),
                pltpu.VMEM((2, nx, HW, co), BF16),
                pltpu.VMEM((2, nx - 1, HW, co), BF16),
                pltpu.VMEM((2, nx, HW, co), BF16),
                pltpu.VMEM((2, nx - 1, HW, co), BF16),
                dma((2,)),
                dma((2, CHUNKS, m - 1)), dma((2, CHUNKS, m - 1)),
                dma((2, CHUNKS, m - 1)), dma((2, CHUNKS, m - 1)),
                dma((2, CHUNKS, 2 * m - 1)), dma((2, CHUNKS, n, k)),
                dma((2, CHUNKS, nx)), dma((2, CHUNKS, nx)),
                dma((2, CHUNKS, nx - 1)), dma((2, CHUNKS, nx - 1)),
            ],
            compiler_params=pltpu.CompilerParams(
                collective_id=0, has_side_effects=True, vmem_limit_bytes=56 * 1024 * 1024
            ),
        )(
            features.reshape(HW, ct),
            kernel_one.reshape(9 * ci, co),
            kernel_two.reshape(9 * ci, co),
        )
        return out.reshape(1, H, W, co)

    placed = (
        P(("groups", "img"), None, None, "chan"),
        P(None, None, "img", "chan"),
        P(None, None, "img", "chan"),
    )
    return jax.shard_map(
        shards,
        mesh=mesh,
        in_specs=placed,
        out_specs=P(("groups", "img"), None, None, "chan"),
        check_vma=False,
    )
```
